256 devices in a mesh: group: 8 (over x, core), dom: 32 (over y, z).
Axes of the slice: x: 4, y: 4, z: 8, core: 2. Of those that a mesh axis runs over, the one named last changes fastest.
Arguments:
- flow_state: float32 [5, 1048576], P(None, ('group', 'dom')), may hold values from -6 to 6
- right_side: float32 [5, 1048576], P(None, ('group', 'dom')), may hold values from -6 to 6
- coupling: float32 [1048576], P(('group', 'dom')), may hold values from 0.03 to 0.3
- pivot_inv: float32 [32, 25, 32768], P(None, None, ('group', 'dom'))
- lower_blocks: float32 [32, 25, 32768], P(None, None, ('group', 'dom'))
- upper_blocks: float32 [32, 25, 32768], P(None, None, ('group', 'dom')), may hold values from -0.15 to 0.15
- face_up: int32 [8, 32, 256], P('group', 'dom'), may hold values from 0 to 4095, as said below
- face_down: int32 [8, 32, 256], P('group', 'dom'), may hold values from 0 to 4095, as said below
- coef_up: float32 [8, 32, 256], P('group', 'dom'), may hold values from 0.1 to 0.5
- coef_down: float32 [8, 32, 256], P('group', 'dom'), may hold values from 0.1 to 0.5
- send_cell: int32 [32, 32768], P(None, ('group', 'dom')), may hold values from 0 to 4095, as said below
- line_src: int32 [32, 32768], P(None, ('group', 'dom')), may hold values from 0 to 8191, as said below
- ret_slot: int32 [32, 32768], P(None, ('group', 'dom')), may hold values from 0 to 4095, as said below
- cell_src: int32 [1048576], P(('group', 'dom')), may hold values from 0 to 8191, as said below
Outputs:
- solution: float32 [5, 1048576], P(None, ('group', 'dom'))
- drive_next: float32 [5, 1048576], P(None, ('group', 'dom'))
The draws below stay inside these ranges and needn't reach their ends.
Inputs may be any that keep to these rules, and one draw needn't show every extreme that they name: Within a group, the cells named by send_cell for all owners together with the own cells named by line_src cover every cell exactly once; for each sender and owner, the first entries, as many as the cells that sender sends that owner (at most 128), are used and the rest are unused; at most 128 cells go from one partition to one other owner, and this is reached for many pairs in every draw; a partition sends none of its cells to itself through send_cell. Each value of line_src, ret_slot and cell_src is consistent with send_cell as stated in the reference program; each owner's line slots take distinct items. `ret_slot`: used entries point at the slot that holds the sent cell. `cell_src`: each cell's value returns to it from the slot that took it. `face_up`: distinct cells within one partition's list. `face_down`: distinct cells within one partition's list.
All inputs are finite; a program needn't handle non-finite values.
Results may differ from the reference program's by a relative error of at most 0.0001.
Values sent between devices are 32-bit elements; how exact they have to be, the bound alone decides.
A program may use at most 192 MiB of HBM per device.

```python
import math
import jax
import jax.numpy as jnp
from jax import lax

NVAR = 5
LINE_CELL_COUNT = 32
LINES_DEV = 128
SWEEPS = 2
GROUPS = 8
DOMAINS = 32
CELLS_DEV = 4096
CAP = 128
FACES = 256
CELLS = 1048576
LINES = 32768


def group_maps(group_key):
    domains = DOMAINS
    cell_count = CELLS_DEV
    capacity = CAP
    pool_base = domains * capacity
    random_keys = [jax.random.fold_in(group_key, i) for i in range(6)]
    dom_ids = jnp.arange(domains, dtype=jnp.int32)
    relabel = jax.random.permutation(random_keys[0], domains).astype(jnp.int32)
    order_pos = jnp.zeros((domains,), jnp.int32).at[relabel].set(dom_ids)
    offset = (order_pos[None, :] - order_pos[:, None]) % domains
    counts = jnp.where(offset % 2 == 1, capacity, capacity // 2)
    counts = jnp.where(offset == 0, 0, counts).astype(jnp.int32)
    counts = counts + jnp.diag(cell_count - counts.sum(axis=1)).astype(jnp.int32)
    starts = jnp.cumsum(counts, axis=1).astype(jnp.int32) - counts
    ends = starts + counts
    ranks = jax.vmap(lambda one_key: jax.random.permutation(one_key, cell_count))(jax.random.split(random_keys[1], domains)).astype(jnp.int32)
    positions = jnp.arange(cell_count, dtype=jnp.int32)
    dest = jnp.sum((ends[:, None, :] <= positions[None, :, None]).astype(jnp.int32), axis=2).astype(jnp.int32)
    within = positions[None, :] - jnp.take_along_axis(starts, dest, axis=1)
    src_rows = dom_ids[:, None]
    cell_dest = jnp.zeros((domains, cell_count), jnp.int32).at[src_rows, ranks].set(dest)
    cell_within = jnp.zeros((domains, cell_count), jnp.int32).at[src_rows, ranks].set(within)
    slot_ids = jnp.arange(capacity, dtype=jnp.int32)
    pick = jnp.minimum(starts[:, :, None] + slot_ids[None, None, :], cell_count - 1)
    chosen = ranks[dom_ids[:, None, None], pick]
    not_self = dom_ids[:, None] != dom_ids[None, :]
    sent = (slot_ids[None, None, :] < counts[:, :, None]) & not_self[:, :, None]
    send_pad = jax.random.randint(random_keys[2], (domains, domains, capacity), 0, cell_count).astype(jnp.int32)
    send_map = jnp.where(sent, chosen, send_pad)
    recv_valid = jnp.transpose(sent, (1, 0, 2)).reshape(domains, pool_base)
    self_valid = cell_dest == dom_ids[:, None]
    valid = jnp.concatenate([recv_valid, self_valid], 1)
    item_count = pool_base + cell_count
    item_keys = jax.vmap(lambda one_key: jax.random.permutation(one_key, item_count))(jax.random.split(random_keys[3], domains)).astype(jnp.int32)
    item_keys = item_keys + jnp.where(valid, 0, item_count).astype(jnp.int32)
    chosen_items = jnp.argsort(item_keys, axis=1, stable=True)[:, :cell_count].astype(jnp.int32)
    slot_of_item = jnp.zeros((domains, item_count), jnp.int32).at[src_rows, chosen_items].set(positions[None, :])
    ret_pad = jax.random.randint(random_keys[4], (domains, pool_base), 0, cell_count).astype(jnp.int32)
    ret_map = jnp.where(recv_valid, slot_of_item[:, :pool_base], ret_pad).reshape(domains, domains, capacity)
    home_map = jnp.where(self_valid, pool_base + slot_of_item[:, pool_base:], cell_dest * capacity + cell_within).astype(jnp.int32)
    return (send_map, chosen_items, ret_map, home_map)


def all_maps(key):

    def one_group(group_id):
        return group_maps(jax.random.fold_in(key, group_id))
    return lax.map(one_group, jnp.arange(GROUPS, dtype=jnp.int32))


def draw_send_cell(key, part):
    send_map = all_maps(jax.random.fold_in(key, 11))[0]
    return jnp.transpose(send_map, (2, 0, 1, 3)).reshape(DOMAINS, GROUPS * DOMAINS * CAP)


def draw_line_src(key, part):
    chosen_items = all_maps(jax.random.fold_in(key, 11))[1]
    shaped = chosen_items.reshape(GROUPS, DOMAINS, LINE_CELL_COUNT, LINES_DEV)
    return jnp.transpose(shaped, (2, 0, 1, 3)).reshape(LINE_CELL_COUNT, GROUPS * DOMAINS * LINES_DEV)


def draw_ret_slot(key, part):
    ret_map = all_maps(jax.random.fold_in(key, 11))[2]
    return jnp.transpose(ret_map, (2, 0, 1, 3)).reshape(DOMAINS, GROUPS * DOMAINS * CAP)


def draw_cell_src(key, part):
    home_map = all_maps(jax.random.fold_in(key, 11))[3]
    return home_map.reshape(-1)


def face_list(key):
    device_keys = jax.random.split(key, GROUPS * DOMAINS)
    picked = jax.vmap(lambda one_key: jax.random.permutation(one_key, CELLS_DEV)[:FACES])(device_keys)
    return picked.astype(jnp.int32).reshape(GROUPS, DOMAINS, FACES)


def draw_face_up(key, part):
    return face_list(jax.random.fold_in(key, 21))


def draw_face_down(key, part):
    return face_list(jax.random.fold_in(key, 22))


def factor_pair(key):
    array_dimensions = (LINE_CELL_COUNT, NVAR * NVAR, LINES)
    random_keys = [jax.random.fold_in(key, i) for i in range(9)]
    entry = lax.broadcasted_iota(jnp.int32, array_dimensions, 1)
    on_diag = entry // NVAR == entry % NVAR
    fast_diag = jax.random.uniform(random_keys[0], array_dimensions, jnp.float32, 0.4, 0.9)
    piv_off = jnp.clip(0.06 * jax.random.normal(random_keys[1], array_dimensions, jnp.float32), -0.15, 0.15)
    slow_share = 0.5
    slow_channel = jax.random.uniform(random_keys[2], (NVAR, LINES), jnp.float32) < slow_share
    slow_entry = jnp.repeat(slow_channel, NVAR, axis=0)[None, :, :]
    slow_diag = jax.random.uniform(random_keys[3], array_dimensions, jnp.float32, 0.9, 1.0)
    piv_diag = jnp.where(slow_entry, slow_diag, fast_diag)
    pivot = jnp.where(on_diag, piv_diag, piv_off)
    sign_pick = jax.random.bernoulli(random_keys[4], 0.5, (1, NVAR * NVAR, LINES))
    signs = jnp.where(sign_pick, 1.0, -1.0).astype(jnp.float32)
    growth_factors = jax.random.uniform(random_keys[5], array_dimensions, jnp.float32, 0.8, 0.92)
    spike_location = jax.random.permutation(random_keys[6], LINE_CELL_COUNT - 1)[:3].astype(jnp.int32) + 1
    cell_position = lax.broadcasted_iota(jnp.int32, (LINE_CELL_COUNT, 1, 1), 0)
    spike_flags = jnp.any(cell_position[..., None] == spike_location[None, None, None, :], axis=-1)
    spike_scale = jax.random.uniform(random_keys[7], array_dimensions, jnp.float32, 0.5, 0.8)
    growth_factors = jnp.where(spike_flags, growth_factors * spike_scale, growth_factors)
    slow_low = signs * growth_factors / slow_diag
    fast_low = jax.random.uniform(random_keys[8], array_dimensions, jnp.float32, -0.15, 0.15)
    low_diag = jnp.where(slow_entry, slow_low, fast_low)
    low_off = 0.08 / 0.15 * jax.random.uniform(jax.random.fold_in(random_keys[8], 5), array_dimensions, jnp.float32, -0.15, 0.15)
    lower = jnp.where(on_diag, low_diag, low_off)
    return (pivot.astype(jnp.float32), lower.astype(jnp.float32))


def draw_pivot_inv(key, part):
    return factor_pair(jax.random.fold_in(key, 31))[0]


def draw_lower_blocks(key, part):
    return factor_pair(jax.random.fold_in(key, 31))[1]


def shard_levels(rng, extent, shards, least, high):
    factor_of, own = 1.0, jax.random.fold_in(rng, 6)
    for position, shards_of in shards:
        heights = jnp.exp(jax.random.uniform(jax.random.fold_in(own, position), (shards_of,), jnp.float32, least / len(shards), high / len(shards)))
        factor_of = factor_of * jnp.repeat(heights, extent[position] // shards_of).reshape([-1 if axis == position else 1 for axis in range(len(extent))])
    return factor_of


def centred(stream_key, shape, deviation, most, cuts=(), kind=jnp.bfloat16):
    gain = shard_levels(stream_key, shape, cuts, -0.22, 0.18) if cuts else 1.0
    array = jax.random.normal(stream_key, shape, jnp.float32) * deviation * gain
    return jnp.minimum(jnp.maximum(array, -most), most).astype(kind)


def setup_inputs(seed: int = 0) -> dict:
    splits = jax.random.split(jax.random.key(seed), 15)
    flow_state = centred(splits[0], (NVAR, CELLS), 1.0, 6.0, ((1, 256),), jnp.float32)
    right_side = centred(splits[1], (NVAR, CELLS), 1.0, 6.0, ((1, 256),), jnp.float32)
    coupling = jnp.clip(jnp.exp(math.log(0.3) - 2.3025852 * jax.random.uniform(splits[2], (CELLS,), jnp.float32) ** shard_levels(splits[2], (CELLS,), ((0, 256),), -0.2, 0.2)), 0.03, 0.3)
    pivot_inv = draw_pivot_inv(jax.random.fold_in(splits[14], 71), 0)
    lower_blocks = draw_lower_blocks(jax.random.fold_in(splits[14], 71), 0)
    upper_blocks = jnp.clip(jax.random.uniform(splits[5], (LINE_CELL_COUNT, NVAR * NVAR, LINES), jnp.float32, -0.15, 0.15) * shard_levels(splits[5], (LINE_CELL_COUNT, NVAR * NVAR, LINES), ((2, 256),), -0.4, 0.0), -0.15, 0.15)
    face_up = draw_face_up(jax.random.fold_in(splits[14], 71), 0)
    face_down = draw_face_down(jax.random.fold_in(splits[14], 71), 0)
    coef_up = jnp.clip(jnp.exp(math.log(0.5) - 1.609438 * jax.random.uniform(splits[8], (GROUPS, DOMAINS, FACES), jnp.float32) ** shard_levels(splits[8], (GROUPS, DOMAINS, FACES), ((0, 8), (1, 32)), -0.2, 0.2)), 0.1, 0.5)
    coef_down = jnp.clip(jnp.exp(math.log(0.5) - 1.609438 * jax.random.uniform(splits[9], (GROUPS, DOMAINS, FACES), jnp.float32) ** shard_levels(splits[9], (GROUPS, DOMAINS, FACES), ((0, 8), (1, 32)), -0.2, 0.2)), 0.1, 0.5)
    send_cell = draw_send_cell(jax.random.fold_in(splits[14], 71), 0)
    line_src = draw_line_src(jax.random.fold_in(splits[14], 71), 0)
    ret_slot = draw_ret_slot(jax.random.fold_in(splits[14], 71), 0)
    cell_src = draw_cell_src(jax.random.fold_in(splits[14], 71), 0)
    return dict(flow_state=flow_state, right_side=right_side, coupling=coupling, pivot_inv=pivot_inv, lower_blocks=lower_blocks, upper_blocks=upper_blocks, face_up=face_up, face_down=face_down, coef_up=coef_up, coef_down=coef_down, send_cell=send_cell, line_src=line_src, ret_slot=ret_slot, cell_src=cell_src)


def reference(flow_state, right_side, coupling, pivot_inv, lower_blocks, upper_blocks, face_up, face_down, coef_up, coef_down, send_cell, line_src, ret_slot, cell_src):
    groups = GROUPS
    domains = DOMAINS
    cell_count = CELLS_DEV
    pool_base = domains * CAP
    nvar = NVAR
    g_idx = jnp.arange(groups, dtype=jnp.int32)[:, None, None]
    d_idx = jnp.arange(domains, dtype=jnp.int32)[None, :, None]
    rhs_grid = right_side.reshape(nvar, groups, domains, cell_count)
    coup_grid = coupling.reshape(groups, domains, cell_count)

    def drive_term(values):
        zeros_col = jnp.zeros((nvar, groups, domains, 1), jnp.float32)
        beside = jnp.concatenate([zeros_col, values[..., :-1]], 3) + jnp.concatenate([values[..., 1:], zeros_col], 3)
        total = rhs_grid + coup_grid[None] * beside
        up_vals = values[:, g_idx, d_idx, face_up]
        down_vals = values[:, g_idx, d_idx, face_down]
        zero_rim = jnp.zeros((nvar, 1, domains, FACES), jnp.float32)
        from_below = jnp.concatenate([zero_rim, up_vals[:, :-1]], 1)
        from_above = jnp.concatenate([down_vals[:, 1:], zero_rim], 1)
        total = total.at[:, g_idx, d_idx, face_down].add(coef_down[None] * from_below)
        total = total.at[:, g_idx, d_idx, face_up].add(coef_up[None] * from_above)
        return total

    send_grid = send_cell.reshape(domains, groups, domains, CAP)
    src_grid = line_src.reshape(LINE_CELL_COUNT, groups, domains, LINES_DEV).transpose(1, 2, 0, 3).reshape(groups, domains, cell_count)
    ret_grid = ret_slot.reshape(domains, groups, domains, CAP)
    home_grid = cell_src.reshape(groups, domains, cell_count)

    def factor_grid(arr):
        return arr.reshape(LINE_CELL_COUNT, nvar, nvar, groups, domains, LINES_DEV)

    pivots = factor_grid(pivot_inv)
    lowers = factor_grid(lower_blocks)
    uppers = factor_grid(upper_blocks)
    high = lax.Precision.HIGHEST

    def solve_lines(line_vals):
        blocks = line_vals.reshape(nvar, groups, domains, LINE_CELL_COUNT, LINES_DEV).transpose(3, 0, 1, 2, 4)

        def forward(prev, inputs):
            rhs_p, piv_p, low_p = inputs
            reduced = rhs_p - jnp.einsum('abgnl,bgnl->agnl', low_p, prev, precision=high)
            result = jnp.einsum('abgnl,bgnl->agnl', piv_p, reduced, precision=high)
            return result, result

        start_vals = jnp.zeros((nvar, groups, domains, LINES_DEV), jnp.float32)
        forward_vals = lax.scan(forward, start_vals, (blocks, pivots, lowers))[1]

        def backward(later, inputs):
            fwd_p, upp_p = inputs
            result = fwd_p - jnp.einsum('abgnl,bgnl->agnl', upp_p, later, precision=high)
            return result, result

        rest = lax.scan(backward, forward_vals[-1], (forward_vals[:-1], uppers[:-1]), reverse=True)[1]
        solved = jnp.concatenate([rest, forward_vals[-1:]], 0)
        return solved.transpose(1, 2, 3, 0, 4).reshape(nvar, groups, domains, cell_count)

    state_now = flow_state.reshape(nvar, groups, domains, cell_count)
    for sweep_idx in range(SWEEPS):
        drive_vals = drive_term(state_now)
        remote = src_grid < pool_base
        clipped = jnp.minimum(src_grid, pool_base - 1)
        source = jnp.where(remote, clipped // CAP, d_idx)
        within = clipped % CAP
        cell_pick = jnp.where(remote, send_grid[d_idx, g_idx, source, within], src_grid - pool_base)
        line_vals = drive_vals[:, g_idx, source, cell_pick]
        solved = solve_lines(line_vals)
        remote_home = home_grid < pool_base
        clip_home = jnp.minimum(home_grid, pool_base - 1)
        owner = jnp.where(remote_home, clip_home // CAP, d_idx)
        within_home = clip_home % CAP
        slot_pick = jnp.where(remote_home, ret_grid[d_idx, g_idx, owner, within_home], home_grid - pool_base)
        state_now = solved[:, g_idx, owner, slot_pick]
    drive_last = drive_term(state_now)
    return state_now.reshape(nvar, -1), drive_last.reshape(nvar, -1)
```

```python
import functools

import jax
import jax.numpy as jnp
from jax import lax
from jax.experimental import pallas as pl
from jax.experimental.pallas import tpu as pltpu
from jax.sharding import PartitionSpec as P

SWEEPS = 2
LANES = 128
SUBLANES = 8
MESH = pl.DeviceIdType.MESH


def bcast(row):
    return jnp.broadcast_to(row, (SUBLANES, LANES))


def lane_pick(row, lane):
    return jnp.take_along_axis(bcast(row), lane, axis=1, mode="promise_in_bounds")


def pick_rows(load_row, row_count, row, lane, start, nvar, unroll=8):
    unroll = min(unroll, row_count)

    def body(step, picked):
        picked = list(picked)
        for u in range(unroll):
            r = step * unroll + u
            hit = row == r
            for v in range(nvar):
                picked[v] = jnp.where(hit, lane_pick(load_row(v, r), lane), picked[v])
        return tuple(picked)

    return lax.fori_loop(0, row_count // unroll, body, tuple(start))


def kernel(
    nvar,
    groups,
    domains,
    flow_ref,
    rhs_ref,
    coup_ref,
    piv_hbm,
    low_hbm,
    upp_hbm,
    face_up_ref,
    face_down_ref,
    coef_up_ref,
    coef_down_ref,
    send_idx_ref,
    line_idx_ref,
    ret_idx_ref,
    cell_idx_ref,
    sol_ref,
    drv_ref,
    state,
    drive,
    rhs,
    lines,
    out_buf,
    in_buf,
    piv,
    low,
    upp,
    face_idx,
    inv,
    face_out,
    face_in,
    factor_sem,
    send_sem,
    recv_sem,
    face_send_sem,
    face_recv_sem,
):
    g = lax.axis_index("group")
    d = lax.axis_index("dom")
    rows = state.shape[1]
    blocks = rows // SUBLANES
    length = piv.shape[0]
    above = lax.rem(g + 1, groups)
    below = lax.rem(g + groups - 1, groups)
    zero = jnp.zeros((SUBLANES, LANES), jnp.float32)
    zeros = [zero] * nvar

    factor_copies = [
        pltpu.make_async_copy(src, dst, factor_sem.at[i])
        for i, (src, dst) in enumerate(((piv_hbm, piv), (low_hbm, low), (upp_hbm, upp)))
    ]
    for copy in factor_copies:
        copy.start()

    barrier = pltpu.get_barrier_semaphore()

    def greet(i, carry):
        peer = lax.rem(d + i, domains)
        pl.semaphore_signal(barrier, inc=1, device_id={"dom": peer}, device_id_type=MESH)
        return carry

    lax.fori_loop(1, domains, greet, 0)
    for peer in (above, below):
        pl.semaphore_signal(barrier, inc=1, device_id={"group": peer}, device_id_type=MESH)

    for r in range(rows):
        part = slice(r * LANES, (r + 1) * LANES)
        state[:, r, :] = flow_ref[:, part]
        rhs[:, r, :] = rhs_ref[:, part]

    face_rows = face_up_ref.shape[2] // LANES
    for first, ref in ((0, face_up_ref), (face_rows, face_down_ref)):
        for j in range(face_rows):
            line = ref[0, 0:1, j * LANES : (j + 1) * LANES]
            face_idx[first + j : first + j + 1, :] = line
            face_idx[2 * face_rows + first + j : 2 * face_rows + first + j + 1, :] = line
    faces = face_rows * LANES
    for which, ref in ((0, face_down_ref), (1, face_up_ref)):
        cells = ref[0, 0:1, :]
        number = (lax.broadcasted_iota(jnp.int32, (1, faces), 1) + 1).astype(jnp.float32)
        row_hot = jnp.where(
            lax.broadcasted_iota(jnp.int32, (rows, faces), 0) == (cells >> 7), number, 0.0
        ).astype(jnp.bfloat16)
        lane_hot = jnp.where(
            lax.broadcasted_iota(jnp.int32, (LANES, faces), 0) == (cells & 127), 1.0, 0.0
        ).astype(jnp.bfloat16)
        found = lax.dot_general(
            row_hot, lane_hot, (((1,), (1,)), ((), ())), preferred_element_type=jnp.float32
        )
        inv[which] = found.astype(jnp.int32)

    def state_row(v, r):
        return state[v, pl.ds(r, 1), :]

    def drive_row(v, r):
        return drive[v, pl.ds(r, 1), :]

    def lines_row(v, r):
        return lines[v, pl.ds(r, 1), :]

    def pick_faces(turn):
        index = face_idx[...]
        picked = pick_rows(state_row, rows, index >> 7, index & 127, zeros, nvar)
        for v in range(nvar):
            face_out[turn, 0, v, 0:face_rows, :] = picked[v][0:face_rows]
            face_out[turn, 1, v, 0:face_rows, :] = picked[v][face_rows : 2 * face_rows]

    def face_copy(turn, way):
        return pltpu.make_async_remote_copy(
            src_ref=face_out.at[turn, way],
            dst_ref=face_in.at[turn, way],
            send_sem=face_send_sem.at[turn, way],
            recv_sem=face_recv_sem.at[turn, way],
            device_id={"group": above if way == 0 else below},
            device_id_type=MESH,
        )

    edge = (g == 0, g == groups - 1)

    def drive_term(turn, write):
        lane_ids = lax.broadcasted_iota(jnp.int32, (rows, LANES), 1)
        row_ids = lax.broadcasted_iota(jnp.int32, (rows, LANES), 0)
        first = (lane_ids == 0) & (row_ids == 0)
        last = (lane_ids == LANES - 1) & (row_ids == rows - 1)
        coup = coup_ref[...]
        for v in range(nvar):
            x = state[v]
            left = pltpu.roll(x, 1, 1)
            left = jnp.where(lane_ids == 0, pltpu.roll(left, 1, 0), left)
            right = pltpu.roll(x, LANES - 1, 1)
            right = jnp.where(lane_ids == LANES - 1, pltpu.roll(right, rows - 1, 0), right)
            beside = jnp.where(first, 0.0, left) + jnp.where(last, 0.0, right)
            drive[v] = rhs[v] + coup * beside
        for way in range(2):
            face_copy(turn, way).wait_recv()
        for way, coef_ref in ((0, coef_down_ref), (1, coef_up_ref)):
            for v in range(nvar):
                for j in range(face_rows):
                    coef = coef_ref[0, 0:1, j * LANES : (j + 1) * LANES]
                    value = coef * face_in[turn, way, v, j : j + 1, :]
                    face_in[turn, way, v, j : j + 1, :] = jnp.where(edge[way], 0.0, value)

        def block(b, carry):
            part = pl.ds(pl.multiple_of(b * SUBLANES, SUBLANES), SUBLANES)
            total = [drive[v, part, :] for v in range(nvar)]
            for way in range(2):
                item = inv[way, part, :] - 1
                row, lane = item >> 7, item & 127
                for v in range(nvar):
                    add = zero
                    for j in range(face_rows):
                        value = face_in[turn, way, v, j : j + 1, :]
                        add = jnp.where(row == j, lane_pick(value, lane), add)
                    total[v] = total[v] + add
            for v in range(nvar):
                write(v, b, part, total[v])
            return carry

        lax.fori_loop(0, blocks, block, 0)

    def write_drive(v, b, part, value):
        drive[v, part, :] = value

    def block_copy(phase, peer, slot, sem):
        return pltpu.make_async_remote_copy(
            src_ref=out_buf.at[phase, peer],
            dst_ref=in_buf.at[phase, slot],
            send_sem=send_sem.at[phase, peer],
            recv_sem=recv_sem.at[phase, sem],
            device_id={"dom": peer},
            device_id_type=MESH,
        )

    def exchange(phase, load_row, index_ref):
        def block(b, carry):
            start = pl.multiple_of(b * SUBLANES, SUBLANES)
            index = index_ref[pl.ds(start, SUBLANES), :]
            picked = pick_rows(load_row, rows, index >> 7, index & 127, zeros, nvar)
            for v in range(nvar):
                for s in range(SUBLANES):
                    out_buf[phase, start + s, v : v + 1, :] = picked[v][s : s + 1]
            return carry

        lax.fori_loop(0, domains // SUBLANES, block, 0)

        def send(i, carry):
            block_copy(phase, lax.rem(d + i, domains), d, d).start()
            return carry

        lax.fori_loop(1, domains, send, 0)

    def receive(phase):
        def wait(i, carry):
            peer = lax.rem(d + i, domains)
            block_copy(phase, peer, peer, peer).wait_recv()
            return carry

        lax.fori_loop(1, domains, wait, 0)

    def merge(phase, load_row, index_ref, out):
        def pool_row(v, r):
            return in_buf[phase, r, v : v + 1, :]

        def own(b, carry):
            part = pl.ds(pl.multiple_of(b * SUBLANES, SUBLANES), SUBLANES)
            index = index_ref[part, :]
            row, lane = (index >> 7) - domains, index & 127
            picked = pick_rows(load_row, rows, row, lane, zeros, nvar)
            for v in range(nvar):
                out[v, part, :] = picked[v]
            return carry

        def pool(b, carry):
            part = pl.ds(pl.multiple_of(b * SUBLANES, SUBLANES), SUBLANES)
            index = index_ref[part, :]
            begin = [out[v, part, :] for v in range(nvar)]
            picked = pick_rows(pool_row, domains, index >> 7, index & 127, begin, nvar)
            for v in range(nvar):
                out[v, part, :] = picked[v]
            return carry

        lax.fori_loop(0, blocks, own, 0)
        receive(phase)
        lax.fori_loop(0, blocks, pool, 0)

    def apply_block(ref, p, vector):
        result = []
        for a in range(nvar):
            terms = [
                bcast(ref[p, a * nvar + b : a * nvar + b + 1, :]) * vector[b] for b in range(nvar)
            ]
            result.append((terms[0] + terms[1]) + (terms[2] + terms[3]) + terms[4])
        return result

    def solve():
        def row_of(p):
            return [bcast(lines[v, pl.ds(p, 1), :]) for v in range(nvar)]

        def put(p, values):
            for v in range(nvar):
                lines[v, pl.ds(p, 1), :] = values[v][0:1]

        first = apply_block(piv, 0, row_of(0))
        put(0, first)

        def forward(p, previous):
            term = apply_block(low, p, previous)
            reduced = [q - t for q, t in zip(row_of(p), term)]
            result = apply_block(piv, p, reduced)
            put(p, result)
            return tuple(result)

        last = lax.fori_loop(1, length, forward, tuple(first))

        def backward(i, later):
            p = length - 2 - i
            term = apply_block(upp, p, later)
            result = [y - t for y, t in zip(row_of(p), term)]
            put(p, result)
            return tuple(result)

        lax.fori_loop(0, length - 1, backward, last)

    pick_faces(0)
    pl.semaphore_wait(barrier, domains + 1)
    for way in range(2):
        face_copy(0, way).start()
    for copy in factor_copies:
        copy.wait()

    for sweep in range(SWEEPS):
        drive_term(sweep, write_drive)
        exchange(2 * sweep, drive_row, send_idx_ref)
        merge(2 * sweep, drive_row, line_idx_ref, lines)
        solve()
        exchange(2 * sweep + 1, lines_row, ret_idx_ref)
        merge(2 * sweep + 1, lines_row, cell_idx_ref, state)
        pick_faces(sweep + 1)
        for way in range(2):
            face_copy(sweep + 1, way).start()
    for r in range(rows):
        sol_ref[:, r * LANES : (r + 1) * LANES] = state[:, r, :]
    drive_term(SWEEPS, write_drive)
    for r in range(rows):
        drv_ref[:, r * LANES : (r + 1) * LANES] = drive[:, r, :]

    for turn in range(SWEEPS + 1):
        for way in range(2):
            face_copy(turn, way).wait_send()

    def drain(i, carry):
        for phase in range(2 * SWEEPS):
            block_copy(phase, lax.rem(d + i, domains), d, d).wait_send()
        return carry

    lax.fori_loop(1, domains, drain, 0)


def shards(*args):
    (flow_state, right_side, coupling, pivot_inv, lower_blocks, upper_blocks, face_up, face_down,
     coef_up, coef_down, send_cell, line_src, ret_slot, cell_src) = args
    nvar, cell_count = flow_state.shape
    rows = cell_count // LANES
    groups, domains = lax.axis_size("group"), lax.axis_size("dom")
    face_rows = face_up.shape[2] // LANES
    vmem = pl.BlockSpec(memory_space=pltpu.VMEM)
    hbm = pl.BlockSpec(memory_space=pl.ANY)
    f32, dma = jnp.float32, pltpu.SemaphoreType.DMA
    grid_field = pltpu.VMEM((nvar, rows, LANES), f32)
    pool = pltpu.VMEM((2 * SWEEPS, domains, nvar, LANES), f32)
    turns = SWEEPS + 1
    out = jax.ShapeDtypeStruct(flow_state.shape, f32)
    return pl.pallas_call(
        functools.partial(kernel, nvar, groups, domains),
        out_shape=(out, out),
        in_specs=[vmem] * 3 + [hbm] * 3 + [vmem] * 8,
        out_specs=(vmem, vmem),
        scratch_shapes=[
            grid_field,
            grid_field,
            grid_field,
            grid_field,
            pool,
            pool,
            pltpu.VMEM(pivot_inv.shape, f32),
            pltpu.VMEM(pivot_inv.shape, f32),
            pltpu.VMEM(pivot_inv.shape, f32),
            pltpu.VMEM((SUBLANES, LANES), jnp.int32),
            pltpu.VMEM((2, rows, LANES), jnp.int32),
            pltpu.VMEM((turns, 2, nvar, SUBLANES, LANES), f32),
            pltpu.VMEM((turns, 2, nvar, SUBLANES, LANES), f32),
            dma((3,)),
            dma((2 * SWEEPS, domains)),
            dma((2 * SWEEPS, domains)),
            dma((turns, 2)),
            dma((turns, 2)),
        ],
        compiler_params=pltpu.CompilerParams(collective_id=0, has_side_effects=True),
        name="relax",
    )(flow_state, right_side, coupling.reshape(rows, LANES), pivot_inv, lower_blocks, upper_blocks,
      face_up, face_down, coef_up, coef_down, send_cell, line_src, ret_slot,
      cell_src.reshape(rows, LANES))


def solution(mesh):
    both = ("group", "dom")
    lead, face = P(None, both), P("group", "dom", None)
    return jax.shard_map(
        shards,
        mesh=mesh,
        in_specs=(lead, lead, P(both)) + (P(None, None, both),) * 3 + (face,) * 4
        + (lead, lead, lead, P(both)),
        out_specs=(lead, lead),
        check_vma=False,
    )
```

```python
import functools

import jax
import jax.numpy as jnp
from jax import lax
from jax.experimental import pallas as pl
from jax.experimental.pallas import tpu as pltpu
from jax.sharding import PartitionSpec as P

SWEEPS = 2
LANES = 128
SUBLANES = 8
UNROLL = 4
MESH = pl.DeviceIdType.MESH


def bcast(row):
    return jnp.broadcast_to(row, (SUBLANES, LANES))


def lane_pick(row, lane):
    return jnp.take_along_axis(row, lane, axis=1, mode="promise_in_bounds")


def ring_order(i):
    return i + i // 2 - 2 * (i // 3)


NEAR_FIRST = (0, 1, 7, 2, 6, 3, 5, 4)


def pick_row(picked, load_row, r, row, lane, nvar):
    hits = [one == r for one in row]
    for v in range(nvar):
        values = bcast(load_row(v, r))
        for b, hit in enumerate(hits):
            at = b * nvar + v
            picked[at] = jnp.where(hit, lane_pick(values, lane[b]), picked[at])


def kernel(
    nvar,
    groups,
    domains,
    flow_hbm,
    rhs_hbm,
    coup_hbm,
    piv_hbm,
    low_hbm,
    upp_hbm,
    face_up_hbm,
    face_down_hbm,
    coef_up_hbm,
    coef_down_hbm,
    send_idx_hbm,
    line_idx_hbm,
    ret_idx_hbm,
    cell_idx_hbm,
    sol_hbm,
    drv_hbm,
    flow_in,
    rhs_in,
    coup_ref,
    piv,
    low,
    upp,
    face_up_ref,
    face_down_ref,
    coef_up_ref,
    coef_down_ref,
    send_idx_ref,
    line_idx_ref,
    ret_idx_ref,
    cell_idx_ref,
    state,
    drive,
    rhs,
    lines,
    out_buf,
    in_buf,
    face_idx,
    inv,
    face_out,
    face_in,
    fetch_sem,
    result_sem,
    send_sem,
    recv_sem,
    face_send_sem,
    face_recv_sem,
):
    g = lax.axis_index("group")
    d = lax.axis_index("dom")
    rows = state.shape[1]
    blocks = rows // SUBLANES
    length = piv.shape[1]
    above = lax.rem(g + 1, groups)
    below = lax.rem(g + groups - 1, groups)
    zero = jnp.zeros((SUBLANES, LANES), jnp.float32)
    tall = domains // SUBLANES
    ring, place = d // SUBLANES, lax.rem(d, SUBLANES)

    sources = (flow_hbm, rhs_hbm, coup_hbm, piv_hbm, low_hbm, upp_hbm, face_up_hbm, face_down_hbm,
               coef_up_hbm, coef_down_hbm, send_idx_hbm, line_idx_hbm, ret_idx_hbm, cell_idx_hbm)
    targets = (flow_in, rhs_in, coup_ref, piv, low, upp, face_up_ref, face_down_ref,
               coef_up_ref, coef_down_ref, send_idx_ref, line_idx_ref, ret_idx_ref, cell_idx_ref)
    fetches = [
        pltpu.make_async_copy(src, dst, fetch_sem.at[i])
        for i, (src, dst) in enumerate(zip(sources, targets))
    ]
    late = (3, 4, 5)
    early = [i for i in range(len(fetches)) if i not in late]

    barrier = pltpu.get_barrier_semaphore()

    def greet(i, carry):
        peer = lax.rem(d + i, domains)
        pl.semaphore_signal(barrier, inc=1, device_id={"dom": peer}, device_id_type=MESH)
        return carry

    for peer in (above, below):
        pl.semaphore_signal(barrier, inc=1, device_id={"group": peer}, device_id_type=MESH)
    for i in early:
        fetches[i].start()
    lax.fori_loop(1, domains, greet, 0)
    for i in late:
        fetches[i].start()
    for i in early:
        fetches[i].wait()

    for r in range(rows):
        part = slice(r * LANES, (r + 1) * LANES)
        state[:, r, :] = flow_in[:, part]
        rhs[:, r, :] = rhs_in[:, part]

    face_rows = face_up_ref.shape[2] // LANES
    for first, ref in ((0, face_up_ref), (face_rows, face_down_ref)):
        for j in range(face_rows):
            line = ref[0, 0:1, j * LANES : (j + 1) * LANES]
            face_idx[first + j : first + j + 1, :] = line
            face_idx[2 * face_rows + first + j : 2 * face_rows + first + j + 1, :] = line
    faces = face_rows * LANES

    def state_row(v, r):
        return state[v, pl.ds(r, 1), :]

    def drive_row(v, r):
        return drive[v, pl.ds(r, 1), :]

    def lines_row(v, r):
        return lines[v, pl.ds(r, 1), :]

    def pick_block(load_row, index):
        picked = [zero] * nvar
        for r in range(rows):
            pick_row(picked, load_row, r, [index >> 7], [index & 127], nvar)
        return picked

    def pick_faces(turn):
        picked = pick_block(state_row, face_idx[...])
        for v in range(nvar):
            face_out[turn, 0, v, :, :] = picked[v][0:face_rows]
            face_out[turn, 1, v, :, :] = picked[v][face_rows : 2 * face_rows]

    def face_copy(turn, way):
        return pltpu.make_async_remote_copy(
            src_ref=face_out.at[turn, way],
            dst_ref=face_in.at[turn, way],
            send_sem=face_send_sem.at[turn, way],
            recv_sem=face_recv_sem.at[turn, way],
            device_id={"group": above if way == 0 else below},
            device_id_type=MESH,
        )

    edge = (g == 0, g == groups - 1)

    def drive_local():
        lane_ids = lax.broadcasted_iota(jnp.int32, (rows, LANES), 1)
        row_ids = lax.broadcasted_iota(jnp.int32, (rows, LANES), 0)
        first = (lane_ids == 0) & (row_ids == 0)
        last = (lane_ids == LANES - 1) & (row_ids == rows - 1)
        coup = coup_ref[...]
        for v in range(nvar):
            x = state[v]
            left = pltpu.roll(x, 1, 1)
            left = jnp.where(lane_ids == 0, pltpu.roll(left, 1, 0), left)
            right = pltpu.roll(x, LANES - 1, 1)
            right = jnp.where(lane_ids == LANES - 1, pltpu.roll(right, rows - 1, 0), right)
            beside = jnp.where(first, 0.0, left) + jnp.where(last, 0.0, right)
            drive[v] = rhs[v] + coup * beside

    def drive_faces(turn):
        for way in range(2):
            face_copy(turn, way).wait_recv()
        tables = []
        for way, coef_ref in ((0, coef_down_ref), (1, coef_up_ref)):
            for j in range(face_rows):
                coef = coef_ref[0, 0:1, j * LANES : (j + 1) * LANES]
                for v in range(nvar):
                    value = coef * face_in[turn, way, v, j : j + 1, :]
                    tables.append(bcast(jnp.where(edge[way], 0.0, value)))
        for b in range(blocks):
            part = slice(b * SUBLANES, (b + 1) * SUBLANES)
            items = [inv[way, part, :] - 1 for way in range(2)]
            for v in range(nvar):
                total = drive[v, part, :]
                for way in range(2):
                    add = zero
                    for j in range(face_rows):
                        table = tables[(way * face_rows + j) * nvar + v]
                        add = jnp.where(
                            (items[way] >> 7) == j, lane_pick(table, items[way] & 127), add
                        )
                    total = total + add
                drive[v, part, :] = total

    def block_copy(phase, peer, slot):
        return pltpu.make_async_remote_copy(
            src_ref=out_buf.at[phase, peer],
            dst_ref=in_buf.at[phase, slot],
            send_sem=send_sem.at[phase, peer],
            recv_sem=recv_sem.at[phase, slot],
            device_id={"dom": peer},
            device_id_type=MESH,
        )

    def exchange(phase, load_row, index_ref):
        def one_ring(i, carry):
            offset = ring_order(tall - 1 - i)
            start = pl.multiple_of(lax.rem(ring + offset, tall) * SUBLANES, SUBLANES)
            picked = pick_block(load_row, index_ref[pl.ds(start, SUBLANES), :])
            for s in range(SUBLANES):
                for v in range(nvar):
                    out_buf[phase, start + s, v : v + 1, :] = picked[v][s : s + 1]
            for step in NEAR_FIRST[:0:-1]:
                block_copy(phase, start + lax.rem(place + step, SUBLANES), d).start()

            @pl.when(offset != 0)
            def _():
                block_copy(phase, start + place, d).start()

            return carry

        lax.fori_loop(0, tall, one_ring, 0)

    def merge(phase, load_row, index_ref, out):
        parts = [slice(b * SUBLANES, (b + 1) * SUBLANES) for b in range(blocks)]
        index = [index_ref[part, :] for part in parts]
        row, lane = [one >> 7 for one in index], [one & 127 for one in index]
        own_row = [one - domains for one in row]

        def pool_row(v, r):
            return in_buf[phase, r, v : v + 1, :]

        def own(step, picked):
            picked = list(picked)
            for u in range(SUBLANES):
                pick_row(picked, load_row, step * SUBLANES + u, own_row, lane, nvar)
            return tuple(picked)

        def pool(i, picked):
            picked = list(picked)
            offset = ring_order(i)
            start = lax.rem(ring + offset, tall) * SUBLANES
            for step in NEAR_FIRST:
                r = start + lax.rem(place + step, SUBLANES)
                if step:
                    block_copy(phase, r, r).wait_recv()
                else:

                    @pl.when(offset != 0)
                    def _():
                        block_copy(phase, r, r).wait_recv()

                pick_row(picked, pool_row, r, row, lane, nvar)
            return tuple(picked)

        picked = lax.fori_loop(0, blocks, own, tuple([zero] * (nvar * blocks)))
        picked = lax.fori_loop(0, tall, pool, picked)
        for b, part in enumerate(parts):
            for v in range(nvar):
                out[v, part, :] = picked[b * nvar + v]

    def apply_block(ref, p, vector):
        result = []
        for a in range(nvar):
            terms = [
                bcast(ref[a * nvar + b, pl.ds(p, 1), :]) * vector[b] for b in range(nvar)
            ]
            result.append((terms[0] + terms[1]) + (terms[2] + terms[3]) + terms[4])
        return result

    def solve():
        def row_of(p):
            return [bcast(lines[v, pl.ds(p, 1), :]) for v in range(nvar)]

        def put(p, values):
            for v in range(nvar):
                lines[v, pl.ds(p, 1), :] = values[v][0:1]

        def forward(step, previous):
            for u in range(UNROLL):
                p = step * UNROLL + u
                term = apply_block(low, p, previous)
                reduced = [q - t for q, t in zip(row_of(p), term)]
                previous = apply_block(piv, p, reduced)
                put(p, previous)
            return tuple(previous)

        def backward(step, later):
            for u in range(UNROLL):
                p = length - 1 - step * UNROLL - u
                term = apply_block(upp, p, later)
                later = [y - t for y, t in zip(row_of(p), term)]
                put(p, later)
            return tuple(later)

        ends = tuple([zero] * nvar)
        lax.fori_loop(0, length // UNROLL, forward, ends)
        lax.fori_loop(0, length // UNROLL, backward, ends)

    pick_faces(0)
    drive_local()
    for which, ref in ((0, face_down_ref), (1, face_up_ref)):
        cells = ref[0, 0:1, :]
        number = (lax.broadcasted_iota(jnp.int32, (1, faces), 1) + 1).astype(jnp.float32)
        row_hot = jnp.where(
            lax.broadcasted_iota(jnp.int32, (rows, faces), 0) == (cells >> 7), number, 0.0
        ).astype(jnp.bfloat16)
        lane_hot = jnp.where(
            lax.broadcasted_iota(jnp.int32, (LANES, faces), 0) == (cells & 127), 1.0, 0.0
        ).astype(jnp.bfloat16)
        found = lax.dot_general(
            row_hot, lane_hot, (((1,), (1,)), ((), ())), preferred_element_type=jnp.float32
        )
        inv[which] = found.astype(jnp.int32)

    pl.semaphore_wait(barrier, domains + 1)
    for way in range(2):
        face_copy(0, way).start()

    for sweep in range(SWEEPS):
        if sweep:
            drive_local()
        drive_faces(sweep)
        exchange(2 * sweep, drive_row, send_idx_ref)
        merge(2 * sweep, drive_row, line_idx_ref, lines)
        if sweep == 0:
            for i in late:
                fetches[i].wait()
        solve()
        exchange(2 * sweep + 1, lines_row, ret_idx_ref)
        merge(2 * sweep + 1, lines_row, cell_idx_ref, state)
        pick_faces(sweep + 1)
        for way in range(2):
            face_copy(sweep + 1, way).start()
    sol_copy = pltpu.make_async_copy(state, sol_hbm, result_sem.at[0])
    sol_copy.start()
    drive_local()
    drive_faces(SWEEPS)
    drv_copy = pltpu.make_async_copy(drive, drv_hbm, result_sem.at[1])
    drv_copy.start()

    for turn in range(SWEEPS + 1):
        for way in range(2):
            face_copy(turn, way).wait_send()

    def drain(i, carry):
        for phase in range(2 * SWEEPS):
            block_copy(phase, lax.rem(d + i, domains), d).wait_send()
        return carry

    lax.fori_loop(1, domains, drain, 0)
    sol_copy.wait()
    drv_copy.wait()


def shards(*args):
    (flow_state, right_side, coupling, pivot_inv, lower_blocks, upper_blocks, face_up, face_down,
     coef_up, coef_down, send_cell, line_src, ret_slot, cell_src) = args
    nvar, cell_count = flow_state.shape
    rows = cell_count // LANES
    groups, domains = lax.axis_size("group"), lax.axis_size("dom")
    face_rows = face_up.shape[2] // LANES
    hbm = pl.BlockSpec(memory_space=pl.ANY)
    f32, dma = jnp.float32, pltpu.SemaphoreType.DMA
    operands = (
        flow_state, right_side, coupling.reshape(rows, LANES),
        jnp.transpose(pivot_inv, (1, 0, 2)), jnp.transpose(lower_blocks, (1, 0, 2)),
        jnp.transpose(upper_blocks, (1, 0, 2)),
        face_up, face_down, coef_up, coef_down, send_cell, line_src, ret_slot,
        cell_src.reshape(rows, LANES),
    )
    field = (nvar, rows, LANES)
    grid_field = pltpu.VMEM(field, f32)
    pool = pltpu.VMEM((2 * SWEEPS, domains, nvar, LANES), f32)
    turns = SWEEPS + 1
    faces = pltpu.VMEM((turns, 2, nvar, face_rows, LANES), f32)
    out = jax.ShapeDtypeStruct(field, f32)
    sol, drv = pl.pallas_call(
        functools.partial(kernel, nvar, groups, domains),
        out_shape=(out, out),
        in_specs=[hbm] * len(operands),
        out_specs=(hbm, hbm),
        scratch_shapes=[pltpu.VMEM(x.shape, x.dtype) for x in operands] + [
            grid_field,
            grid_field,
            grid_field,
            grid_field,
            pool,
            pool,
            pltpu.VMEM((SUBLANES, LANES), jnp.int32),
            pltpu.VMEM((2, rows, LANES), jnp.int32),
            faces,
            faces,
            dma((len(operands),)),
            dma((2,)),
            dma((2 * SWEEPS, domains)),
            dma((2 * SWEEPS, domains)),
            dma((turns, 2)),
            dma((turns, 2)),
        ],
        compiler_params=pltpu.CompilerParams(collective_id=0, has_side_effects=True),
        name="relax",
    )(*operands)
    return sol.reshape(nvar, cell_count), drv.reshape(nvar, cell_count)


def solution(mesh):
    both = ("group", "dom")
    lead, face = P(None, both), P("group", "dom", None)
    return jax.shard_map(
        shards,
        mesh=mesh,
        in_specs=(lead, lead, P(both)) + (P(None, None, both),) * 3 + (face,) * 4
        + (lead, lead, lead, P(both)),
        out_specs=(lead, lead),
        check_vma=False,
    )
```

```python
import functools

import jax
import jax.numpy as jnp
from jax import lax
from jax.experimental import pallas as pl
from jax.experimental.pallas import tpu as pltpu
from jax.sharding import PartitionSpec as P

SWEEPS = 2
LANES = 128
SUBLANES = 8
UNROLL = 8
MESH = pl.DeviceIdType.MESH


def bcast(row):
    return jnp.broadcast_to(row, (SUBLANES, LANES))


def lane_pick(row, lane):
    return jnp.take_along_axis(row, lane, axis=1, mode="promise_in_bounds")


RINGS = (2, 1, 3, 0)


def pick_row(picked, load_row, r, row, lane, nvar):
    hits = [one == r for one in row]
    for v in range(nvar):
        values = bcast(load_row(v, r))
        for b, hit in enumerate(hits):
            at = b * nvar + v
            picked[at] = jnp.where(hit, lane_pick(values, lane[b]), picked[at])


def kernel(
    nvar,
    groups,
    domains,
    flow_hbm,
    rhs_hbm,
    coup_hbm,
    piv_hbm,
    low_hbm,
    upp_hbm,
    face_up_hbm,
    face_down_hbm,
    coef_up_hbm,
    coef_down_hbm,
    send_idx_hbm,
    line_idx_hbm,
    ret_idx_hbm,
    cell_idx_hbm,
    sol_out,
    drv_out,
    flow_in,
    rhs_in,
    coup_ref,
    piv,
    low,
    upp,
    face_up_ref,
    face_down_ref,
    coef_up_ref,
    coef_down_ref,
    send_idx_ref,
    line_idx_ref,
    ret_idx_ref,
    cell_idx_ref,
    state,
    drive,
    rhs,
    lines,
    out_buf,
    in_buf,
    send_map,
    ret_map,
    face_idx,
    inv,
    face_out,
    face_in,
    fetch_sem,
    result_sem,
    send_sem,
    recv_sem,
    face_send_sem,
    face_recv_sem,
):
    g = lax.axis_index("group")
    d = lax.axis_index("dom")
    rows = state.shape[1]
    blocks = rows // SUBLANES
    length = piv.shape[1]
    above = lax.rem(g + 1, groups)
    below = lax.rem(g + groups - 1, groups)
    zero = jnp.zeros((SUBLANES, LANES), jnp.float32)
    tall = domains // SUBLANES
    ring, place = d // SUBLANES, lax.rem(d, SUBLANES)

    sources = (flow_hbm, rhs_hbm, coup_hbm, piv_hbm, low_hbm, upp_hbm, face_up_hbm, face_down_hbm,
               coef_up_hbm, coef_down_hbm, send_idx_hbm, line_idx_hbm, ret_idx_hbm, cell_idx_hbm)
    targets = (flow_in, rhs_in, coup_ref, piv, low, upp, face_up_ref, face_down_ref,
               coef_up_ref, coef_down_ref, send_idx_ref, line_idx_ref, ret_idx_ref, cell_idx_ref)
    fetches = [
        pltpu.make_async_copy(src, dst, fetch_sem.at[i])
        for i, (src, dst) in enumerate(zip(sources, targets))
    ]
    late = (3, 4, 5)
    early = [i for i in range(len(fetches)) if i not in late]

    barrier = pltpu.get_barrier_semaphore()

    def greet(i, carry):
        peer = lax.rem(d + i, domains)
        pl.semaphore_signal(barrier, inc=1, device_id={"dom": peer}, device_id_type=MESH)
        return carry

    for peer in (above, below):
        pl.semaphore_signal(barrier, inc=1, device_id={"group": peer}, device_id_type=MESH)
    for i in early:
        fetches[i].start()
    lax.fori_loop(1, domains, greet, 0)
    for i in late:
        fetches[i].start()
    for i in early:
        fetches[i].wait()

    for r in range(rows):
        part = slice(r * LANES, (r + 1) * LANES)
        state[:, r, :] = flow_in[:, part]
        rhs[:, r, :] = rhs_in[:, part]

    face_rows = face_up_ref.shape[2] // LANES
    for first, ref in ((0, face_up_ref), (face_rows, face_down_ref)):
        for j in range(face_rows):
            line = ref[0, 0:1, j * LANES : (j + 1) * LANES]
            face_idx[first + j : first + j + 1, :] = line
            face_idx[2 * face_rows + first + j : 2 * face_rows + first + j + 1, :] = line
    faces = face_rows * LANES

    def state_row(v, r):
        return state[v, pl.ds(r, 1), :]

    def drive_row(v, r):
        return drive[v, pl.ds(r, 1), :]

    def lines_row(v, r):
        return lines[v, pl.ds(r, 1), :]

    def pick_block(load_row, index):
        picked = [zero] * nvar
        for r in range(rows):
            pick_row(picked, load_row, r, [index >> 7], [index & 127], nvar)
        return picked

    def pick_faces(turn):
        half = rows // 2
        index = face_idx[...]
        low_part = lax.broadcasted_iota(jnp.int32, (SUBLANES, LANES), 0) < SUBLANES // 2
        row, lane = jnp.where(low_part, index >> 7, (index >> 7) - half), index & 127
        picked = [zero] * nvar
        for r in range(half):
            hit = row == r
            for v in range(nvar):
                values = jnp.where(low_part, bcast(state_row(v, r)), bcast(state_row(v, r + half)))
                picked[v] = jnp.where(hit, lane_pick(values, lane), picked[v])
        for v in range(nvar):
            other = pltpu.roll(picked[v], SUBLANES // 2, 0)
            found = jnp.where((index >> 7) < half, picked[v], other)
            face_out[turn, 0, v, :, :] = found[0:face_rows]
            face_out[turn, 1, v, :, :] = found[face_rows : 2 * face_rows]

    def face_copy(turn, way):
        return pltpu.make_async_remote_copy(
            src_ref=face_out.at[turn, way],
            dst_ref=face_in.at[turn, way],
            send_sem=face_send_sem.at[turn, way],
            recv_sem=face_recv_sem.at[turn, way],
            device_id={"group": above if way == 0 else below},
            device_id_type=MESH,
        )

    edge = (g == 0, g == groups - 1)

    def send_faces(turn):
        for way in range(2):
            pl.when(jnp.logical_not(edge[1 - way]))(face_copy(turn, way).start)

    def sent_faces(turn):
        for way in range(2):
            pl.when(jnp.logical_not(edge[1 - way]))(face_copy(turn, way).wait_send)

    def drive_local():
        lane_ids = lax.broadcasted_iota(jnp.int32, (rows, LANES), 1)
        row_ids = lax.broadcasted_iota(jnp.int32, (rows, LANES), 0)
        first = (lane_ids == 0) & (row_ids == 0)
        last = (lane_ids == LANES - 1) & (row_ids == rows - 1)
        coup = coup_ref[...]
        for v in range(nvar):
            x = state[v]
            left = pltpu.roll(x, 1, 1)
            left = jnp.where(lane_ids == 0, pltpu.roll(left, 1, 0), left)
            right = pltpu.roll(x, LANES - 1, 1)
            right = jnp.where(lane_ids == LANES - 1, pltpu.roll(right, rows - 1, 0), right)
            beside = jnp.where(first, 0.0, left) + jnp.where(last, 0.0, right)
            drive[v] = rhs[v] + coup * beside

    def drive_faces(turn):
        for way in range(2):
            pl.when(jnp.logical_not(edge[way]))(face_copy(turn, way).wait_recv)
        tables = []
        for way, coef_ref in ((0, coef_down_ref), (1, coef_up_ref)):
            for j in range(face_rows):
                coef = coef_ref[0, 0:1, j * LANES : (j + 1) * LANES]
                for v in range(nvar):
                    value = coef * face_in[turn, way, v, j : j + 1, :]
                    tables.append(bcast(jnp.where(edge[way], 0.0, value)))
        for b in range(blocks):
            part = slice(b * SUBLANES, (b + 1) * SUBLANES)
            items = [inv[way, part, :] - 1 for way in range(2)]
            for v in range(nvar):
                total = drive[v, part, :]
                for way in range(2):
                    add = zero
                    for j in range(face_rows):
                        table = tables[(way * face_rows + j) * nvar + v]
                        add = jnp.where(
                            (items[way] >> 7) == j, lane_pick(table, items[way] & 127), add
                        )
                    total = total + add
                drive[v, part, :] = total

    def block_copy(phase, peer, out_slot, in_slot):
        return pltpu.make_async_remote_copy(
            src_ref=out_buf.at[phase, out_slot],
            dst_ref=in_buf.at[phase, in_slot],
            send_sem=send_sem.at[phase, out_slot],
            recv_sem=recv_sem.at[phase, in_slot],
            device_id={"dom": peer},
            device_id_type=MESH,
        )

    def members(i, sign):
        found = []
        for there in (4 + i, 3 - i):
            for over in RINGS:
                at = lax.rem(place + SUBLANES + sign * there, SUBLANES)
                found.append(lax.rem(ring + tall + sign * over, tall) * SUBLANES + at)
        return found

    def unless_self(i, u, action):
        if u < SUBLANES - 1:
            action()
        else:
            pl.when(i != tall - 1)(action)

    def exchange(phase, load_row, index_ref):
        def one_group(i, carry):
            start = pl.multiple_of(i * SUBLANES, SUBLANES)
            picked = pick_block(load_row, index_ref[pl.ds(start, SUBLANES), :])
            for s in range(SUBLANES):
                for v in range(nvar):
                    out_buf[phase, start + s, v : v + 1, :] = picked[v][s : s + 1]
            for u, peer in enumerate(members(i, 1)):
                unless_self(i, u, block_copy(phase, peer, start + u, d).start)
            return carry

        lax.fori_loop(0, tall, one_group, 0)

    def drain(phase):
        def one_group(i, carry):
            for u, peer in enumerate(members(i, 1)):
                unless_self(i, u, block_copy(phase, peer, i * SUBLANES + u, d).wait_send)
            return carry

        lax.fori_loop(0, tall, one_group, 0)

    def merge(phase, load_row, index_ref, out):
        parts = [slice(b * SUBLANES, (b + 1) * SUBLANES) for b in range(blocks)]

        def pool_row(v, r):
            return in_buf[phase, r, v : v + 1, :]

        def own(b, carry):
            part = pl.ds(pl.multiple_of(b * SUBLANES, SUBLANES), SUBLANES)
            picked = pick_block(load_row, index_ref[part, :] - domains * LANES)
            for v in range(nvar):
                out[v, part, :] = picked[v]
            return carry

        lax.fori_loop(0, blocks, own, 0)
        if phase:
            drain(phase - 1)
        index = [index_ref[part, :] for part in parts]
        row, lane = [one >> 7 for one in index], [one & 127 for one in index]

        def pool(step, picked):
            picked = list(picked)
            i = tall - 1 - step
            peers = members(i, -1)
            for u, peer in enumerate(peers):
                unless_self(i, u, block_copy(phase, peer, peer, peer).wait_recv)
            for b in range(blocks):
                mine = picked[b * nvar : (b + 1) * nvar]
                for peer in peers:
                    pick_row(mine, pool_row, peer, row[b : b + 1], lane[b : b + 1], nvar)
                picked[b * nvar : (b + 1) * nvar] = mine
            return tuple(picked)

        picked = tuple(out[v, part, :] for part in parts for v in range(nvar))
        picked = lax.fori_loop(0, tall, pool, picked)
        for b, part in enumerate(parts):
            for v in range(nvar):
                out[v, part, :] = picked[b * nvar + v]

    def apply_block(ref, p, vector):
        result = []
        for a in range(nvar):
            terms = [
                bcast(ref[a * nvar + b, pl.ds(p, 1), :]) * vector[b] for b in range(nvar)
            ]
            result.append((terms[0] + terms[1]) + (terms[2] + terms[3]) + terms[4])
        return result

    def solve():
        def row_of(p):
            return [bcast(lines[v, pl.ds(p, 1), :]) for v in range(nvar)]

        def put(p, values):
            for v in range(nvar):
                lines[v, pl.ds(p, 1), :] = values[v][0:1]

        def forward(step, previous):
            for u in range(UNROLL):
                p = step * UNROLL + u
                term = apply_block(low, p, previous)
                reduced = [q - t for q, t in zip(row_of(p), term)]
                previous = apply_block(piv, p, reduced)
                put(p, previous)
            return tuple(previous)

        def backward(step, later):
            for u in range(UNROLL):
                p = length - 1 - step * UNROLL - u
                term = apply_block(upp, p, later)
                later = [y - t for y, t in zip(row_of(p), term)]
                put(p, later)
            return tuple(later)

        ends = tuple([zero] * nvar)
        lax.fori_loop(0, length // UNROLL, forward, ends)
        lax.fori_loop(0, length // UNROLL, backward, ends)

    def order_maps(i, carry):
        for u, peer in enumerate(members(i, 1)):
            for ref, ordered in ((send_idx_ref, send_map), (ret_idx_ref, ret_map)):
                ordered[pl.ds(i * SUBLANES + u, 1), :] = ref[pl.ds(peer, 1), :]
        return carry

    pick_faces(0)
    drive_local()
    lax.fori_loop(0, tall, order_maps, 0)
    for which, ref in ((0, face_down_ref), (1, face_up_ref)):
        cells = ref[0, 0:1, :]
        number = (lax.broadcasted_iota(jnp.int32, (1, faces), 1) + 1).astype(jnp.float32)
        row_hot = jnp.where(
            lax.broadcasted_iota(jnp.int32, (rows, faces), 0) == (cells >> 7), number, 0.0
        ).astype(jnp.bfloat16)
        lane_hot = jnp.where(
            lax.broadcasted_iota(jnp.int32, (LANES, faces), 0) == (cells & 127), 1.0, 0.0
        ).astype(jnp.bfloat16)
        found = lax.dot_general(
            row_hot, lane_hot, (((1,), (1,)), ((), ())), preferred_element_type=jnp.float32
        )
        inv[which] = found.astype(jnp.int32)

    pl.semaphore_wait(barrier, domains + 1)
    send_faces(0)

    for sweep in range(SWEEPS):
        if sweep:
            drive_local()
        drive_faces(sweep)
        exchange(2 * sweep, drive_row, send_map)
        merge(2 * sweep, drive_row, line_idx_ref, lines)
        if sweep == 0:
            for i in late:
                fetches[i].wait()
        solve()
        exchange(2 * sweep + 1, lines_row, ret_map)
        merge(2 * sweep + 1, lines_row, cell_idx_ref, state)
        pick_faces(sweep + 1)
        send_faces(sweep + 1)
    sol_copy = pltpu.make_async_copy(state, sol_out, result_sem.at[0])
    sol_copy.start()
    drive_local()
    drain(2 * SWEEPS - 1)
    for turn in range(SWEEPS):
        sent_faces(turn)
    drive_faces(SWEEPS)
    drv_copy = pltpu.make_async_copy(drive, drv_out, result_sem.at[1])
    drv_copy.start()

    sent_faces(SWEEPS)
    sol_copy.wait()
    drv_copy.wait()


def shards(*args):
    (flow_state, right_side, coupling, pivot_inv, lower_blocks, upper_blocks, face_up, face_down,
     coef_up, coef_down, send_cell, line_src, ret_slot, cell_src) = args
    nvar, cell_count = flow_state.shape
    rows = cell_count // LANES
    groups, domains = lax.axis_size("group"), lax.axis_size("dom")
    face_rows = face_up.shape[2] // LANES
    hbm = pl.BlockSpec(memory_space=pl.ANY)
    f32, dma = jnp.float32, pltpu.SemaphoreType.DMA
    operands = (
        flow_state, right_side, coupling.reshape(rows, LANES),
        jnp.transpose(pivot_inv, (1, 0, 2)), jnp.transpose(lower_blocks, (1, 0, 2)),
        jnp.transpose(upper_blocks, (1, 0, 2)),
        face_up, face_down, coef_up, coef_down, send_cell, line_src, ret_slot,
        cell_src.reshape(rows, LANES),
    )
    field = (nvar, rows, LANES)
    grid_field = pltpu.VMEM(field, f32)
    pool = pltpu.VMEM((2 * SWEEPS, domains, nvar, LANES), f32)
    turns = SWEEPS + 1
    faces = pltpu.VMEM((turns, 2, nvar, face_rows, LANES), f32)
    out = pltpu.VMEM(field, f32)
    sol, drv = pl.pallas_call(
        functools.partial(kernel, nvar, groups, domains),
        out_shape=(out, out),
        in_specs=[hbm] * len(operands),
        out_specs=(hbm, hbm),
        scratch_shapes=[pltpu.VMEM(x.shape, x.dtype) for x in operands] + [
            grid_field,
            grid_field,
            grid_field,
            grid_field,
            pool,
            pool,
            pltpu.VMEM(send_cell.shape, jnp.int32),
            pltpu.VMEM(send_cell.shape, jnp.int32),
            pltpu.VMEM((SUBLANES, LANES), jnp.int32),
            pltpu.VMEM((2, rows, LANES), jnp.int32),
            faces,
            faces,
            dma((len(operands),)),
            dma((2,)),
            dma((2 * SWEEPS, domains)),
            dma((2 * SWEEPS, domains)),
            dma((turns, 2)),
            dma((turns, 2)),
        ],
        compiler_params=pltpu.CompilerParams(collective_id=0, has_side_effects=True),
        name="relax",
    )(*operands)
    return sol.reshape(nvar, cell_count), drv.reshape(nvar, cell_count)


def solution(mesh):
    both = ("group", "dom")
    lead, face = P(None, both), P("group", "dom", None)
    return jax.shard_map(
        shards,
        mesh=mesh,
        in_specs=(lead, lead, P(both)) + (P(None, None, both),) * 3 + (face,) * 4
        + (lead, lead, lead, P(both)),
        out_specs=(lead, lead),
        check_vma=False,
    )
```
